256 devices in a mesh: segment: 4 (over x), gz: 64 (over y, z, core).
Axes of the slice: x: 4, y: 4, z: 8, core: 2. Of those that a mesh axis runs over, the one named last changes fastest.
Arguments:
- start_volume: float32 [4, 1024, 1024], P(None, 'gz'), may hold values from -6 to 6
- sinogram: float32 [4, 1024, 1024], P(None, 'gz'), may hold values from -6 to 6
- offsets: int32 [4, 8], replicated, may hold values from -15 to 15, as said below
- projector: bfloat16 [3, 1024, 1024], replicated, may hold values from -0.109375 to 0.109375
- dual_in: bfloat16 [32, 27], replicated, may hold values from -1.25 to 1.25
- dual_out: bfloat16 [9, 32], replicated, may hold values from -0.375 to 0.375
- primal_in: bfloat16 [64, 54], replicated, may hold values from -0.875 to 0.875
- primal_out: bfloat16 [27, 64], replicated, may hold values from -0.15625 to 0.15625
Outputs:
- volume: float32 [4, 1024, 1024], P('segment', 'gz')
The draws below stay inside these ranges and needn't reach their ends.
Inputs may be any that keep to these rules, and one draw needn't show every extreme that they name: `offsets`: both ends of the range are taken in every draw.
All inputs are finite; a program needn't handle non-finite values.
Results may differ from the reference program's by a relative error of at most 0.005.
Values may be sent and summed in bfloat16 or wider, within the bound.
A program may use at most 64 MiB of HBM per device.

```python
import jax
import jax.numpy as jnp
from jax import lax

ZL = 16
IMG = 32
NCOL = 128
VIEWS = 8
DUAL_CH = 32
PRIMAL_CH = 64
ITERS = 2
SLABS = 4
Z = 1024
CELLS = 1024


def draw_offsets(key, part):
    key_values = jax.random.fold_in(key, 11)
    key_places = jax.random.fold_in(key, 23)
    drawn = jax.random.randint(key_values, (SLABS * VIEWS,), -(ZL - 1), ZL, dtype=jnp.int32)
    order = jax.random.permutation(key_places, SLABS * VIEWS)
    drawn = drawn.at[order[0]].set(ZL - 1)
    drawn = drawn.at[order[1]].set(-(ZL - 1))
    return drawn.reshape(SLABS, VIEWS)


def steps_of(own_key, shape, cuts, low, largest):
    factor_of = 1.0
    for position, shards_of in cuts:
        heights = jax.random.uniform(jax.random.fold_in(jax.random.fold_in(own_key, 6), position), (shards_of,), jnp.float32, low / len(cuts), largest / len(cuts))
        factor_of = factor_of * jnp.repeat(jnp.exp(heights), shape[position] // shards_of).reshape((-1,) + (1,) * (len(shape) - 1 - position))
    return factor_of


def normal_values(stream_key, extent, width, limit, cuts=(), held_as=jnp.bfloat16):
    values = jax.random.normal(stream_key, extent, jnp.float32) * width
    if len(cuts) > 0:
        values = steps_of(stream_key, extent, cuts, -0.22, 0.18) * values
    return jnp.clip(values, min=-limit, max=limit).astype(held_as)


def setup_inputs(seed: int = 0) -> dict:
    seeds = jax.random.split(jax.random.key(seed), 9)
    return {
        "start_volume": normal_values(seeds[0], (SLABS, Z, CELLS), 1.0, 6.0, ((1, 64),), jnp.float32),
        "sinogram": normal_values(seeds[1], (SLABS, Z, CELLS), 1.0, 6.0, ((1, 64),), jnp.float32),
        "offsets": draw_offsets(jax.random.fold_in(seeds[8], 71), 0),
        "projector": normal_values(seeds[3], (3, CELLS, CELLS), (3 * CELLS) ** -0.5, 0.109375),
        "dual_in": normal_values(seeds[4], (DUAL_CH, 27), 27 ** -0.5, 1.25),
        "dual_out": normal_values(seeds[5], (9, DUAL_CH), (9 * DUAL_CH) ** -0.5, 0.375),
        "primal_in": normal_values(seeds[6], (PRIMAL_CH, 54), 54 ** -0.5, 0.875),
        "primal_out": normal_values(seeds[7], (27, PRIMAL_CH), (27 * PRIMAL_CH) ** -0.5, 0.15625),
    }


def plane_taps(flavour):
    cell_count = IMG * IMG
    positions = jnp.arange(cell_count, dtype=jnp.int32)
    tap_list = []
    if flavour == 0:
        column_of = positions % NCOL
        for step_size in (-1, 0, 1):
            keep_mask = ((column_of + step_size >= 0) & (column_of + step_size < NCOL)).astype(jnp.float32)
            tap_list.append((step_size, keep_mask))
    else:
        row_of = positions // IMG
        column_of = positions % IMG
        for down_step in (-1, 0, 1):
            for across_step in (-1, 0, 1):
                keep_mask = ((row_of + down_step >= 0) & (row_of + down_step < IMG) & (column_of + across_step >= 0) & (column_of + across_step < IMG)).astype(jnp.float32)
                tap_list.append((down_step * IMG + across_step, keep_mask))
    return tap_list


def plane_shift(values, offset, keep_mask):
    margin = IMG + 1
    cell_count = values.shape[-1]
    widths = [(0, 0)] * (values.ndim - 1) + [(margin, margin)]
    padded = jnp.pad(values, widths)
    shifted = lax.slice_in_dim(padded, margin + offset, margin + offset + cell_count, axis=values.ndim - 1)
    return shifted * keep_mask.astype(values.dtype)


def expand(source, row_count, tap_list):
    pieces = []
    for depth_index in range(3):
        layer_rows = lax.slice_in_dim(source, depth_index, depth_index + row_count, axis=1)
        for offset, keep_mask in tap_list:
            pieces.append(plane_shift(layer_rows, offset, keep_mask))
    return jnp.concatenate(pieces, axis=0)


def collapse(hidden, w_second, row_count, tap_list):
    partial_value = jnp.einsum("to,ozn->tzn", w_second, hidden)
    summed = jnp.zeros((row_count, hidden.shape[2]), jnp.float32)
    tap_number = 0
    for depth_index in range(3):
        for offset, keep_mask in tap_list:
            layer_rows = lax.slice_in_dim(partial_value[tap_number], depth_index, depth_index + row_count, axis=0)
            summed = summed + plane_shift(layer_rows, offset, keep_mask)
            tap_number = tap_number + 1
    return summed


def network(channels, w_in, w_out, tap_list):
    total_rows = channels.shape[1]
    rounded = lax.optimization_barrier(channels.astype(jnp.bfloat16)).astype(jnp.float32)
    padded = jnp.pad(rounded, ((0, 0), (2, 2), (0, 0)))
    w_first = w_in.astype(jnp.float32)
    w_second = w_out.astype(jnp.float32)

    def one_block(start_row):
        source = lax.dynamic_slice_in_dim(padded, start_row, ZL + 4, 1)
        columns = expand(source, ZL + 2, tap_list)
        hidden = jax.nn.relu(jnp.einsum("ok,kzn->ozn", w_first, columns))
        hidden = lax.optimization_barrier(hidden.astype(jnp.bfloat16)).astype(jnp.float32)
        global_row = start_row - 1 + jnp.arange(ZL + 2, dtype=jnp.int32)
        inside = ((global_row >= 0) & (global_row < total_rows)).astype(jnp.float32)
        hidden = hidden * inside[None, :, None]
        return collapse(hidden, w_second, ZL, tap_list)

    starts = jnp.arange(total_rows // ZL, dtype=jnp.int32) * ZL
    blocks = lax.map(one_block, starts)
    return blocks.reshape(total_rows, channels.shape[2])


def band_full(values, shifts, projector, adjoint):
    row_count = values.shape[0]
    cell_count = values.shape[1]
    groups = shifts.shape[0]
    group_width = cell_count // groups
    rounded = lax.optimization_barrier(values.astype(jnp.bfloat16)).astype(jnp.float32)
    padded = jnp.pad(rounded, ((ZL, ZL), (0, 0)))
    weights = projector.astype(jnp.float32)
    if adjoint:
        starts = (ZL - 1 - shifts).astype(jnp.int32)
        grouped = padded.reshape(padded.shape[0], groups, group_width)
        windows = jax.vmap(lambda column, start_row: lax.dynamic_slice_in_dim(column, start_row, row_count + 2, 0), in_axes=(1, 0))(grouped, starts)
        summed = jnp.zeros((row_count, cell_count), jnp.float32)
        for tap_row in range(3):
            window_rows = lax.slice_in_dim(windows, 2 - tap_row, 2 - tap_row + row_count, axis=1)
            summed = summed + jnp.einsum("gzc,pgc->zp", window_rows, weights[tap_row].reshape(cell_count, groups, group_width))
        return summed
    starts = (ZL - 1 + shifts).astype(jnp.int32)
    windows = jax.vmap(lambda start_row: lax.dynamic_slice_in_dim(padded, start_row, row_count + 2, 0))(starts)
    by_group = jnp.zeros((row_count, groups, group_width), jnp.float32)
    for tap_row in range(3):
        window_rows = lax.slice_in_dim(windows, tap_row, tap_row + row_count, axis=1)
        by_group = by_group + jnp.einsum("gzp,pgc->zgc", window_rows, weights[tap_row].reshape(cell_count, groups, group_width))
    return by_group.reshape(row_count, cell_count)


def reference(start_volume, sinogram, offsets, projector, dual_in, dual_out, primal_in, primal_out):
    dual_taps = plane_taps(0)
    primal_taps = plane_taps(1)
    results = []
    for slab_index in range(SLABS):
        current = start_volume[slab_index]
        dual_state = jnp.zeros_like(current)
        for rounds in range(ITERS):
            forward = band_full(current, offsets[slab_index], projector, False)
            dual_state = dual_state + network(jnp.stack([dual_state, forward, sinogram[slab_index]]), dual_in, dual_out, dual_taps)
            backward = band_full(dual_state, offsets[slab_index], projector, True)
            current = current + network(jnp.stack([current, backward]), primal_in, primal_out, primal_taps)
        results.append(current)
    return jnp.stack(results)
```

```python
import functools

import jax
import jax.numpy as jnp
from jax import lax
from jax.experimental import pallas as pl
from jax.experimental.pallas import tpu as pltpu
from jax.sharding import PartitionSpec as P

IMG = 32
NCOL = 128
ITERS = 2
BF = jnp.bfloat16
F32 = jnp.float32
MESH = pl.DeviceIdType.MESH

BASE = 24
GROUPS = 3
STEP = 6


def iota(shape, dim):
    return lax.broadcasted_iota(jnp.int32, shape, dim)


def one_hot(mask):
    return jnp.where(mask, 1.0, 0.0).astype(BF)


def dot(a, b):
    return jnp.dot(a, b, preferred_element_type=F32)


def dual_keep(step, width):
    col = iota((1, width), 1) % NCOL + step
    return (col >= 0) & (col < NCOL)


def primal_keep(down, across, width):
    lane = iota((1, width), 1)
    row = lane // IMG + down
    col = lane % IMG + across
    return (row >= 0) & (row < IMG) & (col >= 0) & (col < IMG)


def shifted(x, offset, keep):
    if offset == 0:
        return x
    width = x.shape[-1]
    return jnp.where(keep, pltpu.roll(x, (-offset) % width, 1), 0.0)


def first_weights(w, taps, rows_in_k, out_ref):
    for z in range(STEP):
        q = iota((3 * taps, rows_in_k), 0)
        c = iota((3 * taps, rows_in_k), 1)
        zz = c % 8
        j = c // 8
        sel = one_hot((q == (zz - z) * taps + j) & (j < taps))
        count = w.shape[0]
        out_ref[z * count : (z + 1) * count, :] = dot(w, sel).astype(BF)


def second_weights(w, taps, row_count, first_row, total_rows, out_ref):
    count = w.shape[1]
    pack = 128 // count
    q = iota((pack * 3 * taps, 3 * taps), 0)
    t = iota((pack * 3 * taps, 3 * taps), 1)
    stacked = dot(one_hot(q % (3 * taps) == t), w).astype(BF)
    spread = one_hot(iota((count, 128), 0) == iota((count, 128), 1) % count)
    wide = dot(stacked, spread)
    qq = iota(wide.shape, 0) // (3 * taps)
    lane = iota(wide.shape, 1) // count
    wide = jnp.where(qq == lane, wide, 0.0).astype(BF)
    height = taps * row_count
    hidden_rows = row_count + 2
    for m in range(-(-hidden_rows // pack)):
        r = iota((height, pack * 3 * taps), 0)
        c = iota((height, pack * 3 * taps), 1)
        y = m * pack + c // (3 * taps)
        row = first_row + y - 1
        mask = (c % (3 * taps)) == (y - r % row_count) * taps + r // row_count
        mask = mask & (y < hidden_rows) & (row >= 0) & (row < total_rows)
        out_ref[:, m * 128 : (m + 1) * 128] = dot(one_hot(mask), wide).astype(BF)


def kernel(
    sizes,
    sv_hbm,
    sino_hbm,
    off_ref,
    proj_hbm,
    din_hbm,
    dout_hbm,
    pin_hbm,
    pout_hbm,
    out_ref,
    field,
    sino,
    dual,
    proj,
    din,
    dout,
    pin,
    pout,
    ext,
    far_s,
    far_r,
    sino_s,
    sino_r,
    far_f,
    g,
    u,
    xf,
    xs,
    xa,
    wd,
    vd,
    wp,
    vp,
    cold,
    colp,
    hid,
    res,
    load_sem,
    send_sem,
    recv_sem,
    sino_ssem,
    sino_rsem,
):
    seg_count, gz_count, rows, cells = sizes
    views = cells // NCOL
    total = gz_count * rows
    seg = lax.axis_index("segment")
    me = lax.axis_index("gz")
    right = lax.rem(me + 1, gz_count)
    left = lax.rem(me + gz_count - 1, gz_count)
    right2 = lax.rem(me + 2, gz_count)
    left2 = lax.rem(me + gz_count - 2, gz_count)
    first_row = me * rows

    barrier = pltpu.get_barrier_semaphore()
    for other in (left, right, left2, right2):
        pl.semaphore_signal(barrier, inc=1, device_id={"gz": other}, device_id_type=MESH)

    loads = [
        pltpu.make_async_copy(src, dst, load_sem.at[i])
        for i, (src, dst) in enumerate(
            [
                (sv_hbm.at[seg], field),
                (sino_hbm.at[seg], sino),
                (din_hbm, din),
                (dout_hbm, dout),
                (pin_hbm, pin),
                (pout_hbm, pout),
                (proj_hbm, proj),
            ]
        )
    ]
    for copy in loads:
        copy.start()

    def remote(src, dst, ssem, rsem, other):
        return pltpu.make_async_remote_copy(
            src_ref=src,
            dst_ref=dst,
            send_sem=ssem,
            recv_sem=rsem,
            device_id={"gz": other},
            device_id_type=MESH,
        )

    def copies(e):
        own = ext.at[e, pl.ds(16, 16)]
        return [
            remote(own, ext.at[e, pl.ds(0, 16)], send_sem.at[e, 0], recv_sem.at[e, 0], right),
            remote(own, ext.at[e, pl.ds(32, 16)], send_sem.at[e, 1], recv_sem.at[e, 1], left),
            remote(far_s.at[e, 1], far_r.at[e, 0], send_sem.at[e, 2], recv_sem.at[e, 2], right2),
            remote(far_s.at[e, 0], far_r.at[e, 1], send_sem.at[e, 3], recv_sem.at[e, 3], left2),
        ]

    def send(e, ref):
        ext[e, 16:32, :] = ref[...].astype(BF)
        far_s[e, 0] = ref[0:2, :].astype(BF)
        far_s[e, 1] = ref[rows - 2 : rows, :].astype(BF)
        for copy in copies(e):
            copy.start()

    def receive(e):
        for copy in copies(e):
            copy.wait()

        @pl.when(me == 0)
        def _():
            ext[e, 0:16, :] = jnp.zeros((16, cells), BF)

        @pl.when(me == gz_count - 1)
        def _():
            ext[e, 32:48, :] = jnp.zeros((16, cells), BF)

        @pl.when(me <= 1)
        def _():
            far_r[e, 0] = jnp.zeros((2, cells), BF)

        @pl.when(me >= gz_count - 2)
        def _():
            far_r[e, 1] = jnp.zeros((2, cells), BF)

    sino_copies = [
        remote(sino_s.at[1], sino_r.at[0], sino_ssem.at[0], sino_rsem.at[0], right),
        remote(sino_s.at[0], sino_r.at[1], sino_ssem.at[1], sino_rsem.at[1], left),
    ]

    loads[0].wait()
    loads[1].wait()
    sino_s[0] = sino[0:2, :].astype(BF)
    sino_s[1] = sino[rows - 2 : rows, :].astype(BF)
    pl.semaphore_wait(barrier, 4)
    send(0, field)
    for copy in sino_copies:
        copy.start()

    u[...] = jnp.zeros(u.shape, F32)
    far_f[...] = jnp.zeros(far_f.shape, F32)
    for k in range(3):
        g[k, :, 0:8, :] = jnp.zeros((views, 8, NCOL), F32)
        g[k, :, 56:64, :] = jnp.zeros((views, 8, NCOL), F32)
    hid[576:640, :] = jnp.zeros((64, hid.shape[1]), BF)
    dual[...] = jnp.zeros(dual.shape, F32)
    for i in range(2, 6):
        loads[i].wait()
    first_weights(din[...], 9, wd.shape[1], wd)
    first_weights(pin[...], 18, wp.shape[1], wp)
    second_weights(dout[...], 3, rows, first_row, total, vd)
    second_weights(pout[...], 9, rows, first_row, total, vp)

    for copy in sino_copies:
        copy.wait()
    xs[2 : 2 + rows, :] = sino[...]
    xs[0:2, :] = jnp.where(me == 0, 0.0, sino_r[0].astype(F32))
    xs[rows + 2 : rows + 4, :] = jnp.where(me == gz_count - 1, 0.0, sino_r[1].astype(F32))
    loads[6].wait()

    row = iota((24, 1), 0)
    inside = (row < rows + 4) & (first_row + row >= 2) & (first_row + row - 2 < total)

    def network(x_reads, steps, keeps, per_step, w_ref, col, v_ref, out_count):
        pad = w_ref.shape[1] - len(steps) * per_step
        for t in range(GROUPS):
            stack = jnp.concatenate([read(t * STEP) for read in x_reads], 0)
            pieces = [shifted(stack, offset, keep) for offset, keep in zip(steps, keeps)]
            if pad:
                pieces.append(jnp.zeros((pad, cells), F32))
            col[t] = jnp.concatenate(pieces, 0).astype(BF)
        height = w_ref.shape[0]
        depth = v_ref.shape[1]
        out_rows = v_ref.shape[0]
        for n in range(cells // 256):
            lanes = slice(n * 256, (n + 1) * 256)
            for t in range(GROUPS):
                value = dot(w_ref[...], col[t, :, lanes])
                hid[t * height : (t + 1) * height, :] = jnp.maximum(value, 0.0).astype(BF)
            res[0:out_rows, lanes] = dot(v_ref[...], hid[0:depth, :])
        total_value = None
        for s, (offset, keep) in enumerate(zip(steps, keeps)):
            part = shifted(res[s * rows : (s + 1) * rows, :], offset, keep)
            total_value = part if total_value is None else total_value + part
        return total_value

    def rows_of(ref):
        return lambda start: ref[start : start + 8, :]

    def read_u(start):
        low = BASE - 2 + start
        return jnp.concatenate([u[w, low : low + 8, :] for w in range(views)], 1)

    dual_steps = [-1, 0, 1]
    dual_keeps = [dual_keep(s, cells) for s in dual_steps]
    primal_pairs = [(dy, dx) for dy in (-1, 0, 1) for dx in (-1, 0, 1)]
    primal_steps = [dy * IMG + dx for dy, dx in primal_pairs]
    primal_keeps = [primal_keep(dy, dx, cells) for dy, dx in primal_pairs]

    def iteration(it, carry):
        ef = 2 * it
        eh = 2 * it + 1
        receive(ef)
        far_f[0:2, :] = far_r[ef, 0].astype(F32)
        far_f[2:4, :] = far_r[ef, 1].astype(F32)
        ext[ef, 48:64, :] = far_f[...].astype(BF)
        for k in range(3):
            product = dot(ext[ef], proj[k])
            for w in range(views):
                lanes = slice(w * NCOL, (w + 1) * NCOL)
                g[k, w, 8:56, :] = product[0:48, lanes]
                g[k, w, 6:8, :] = product[48:50, lanes]
                g[k, w, 56:58, :] = product[50:52, lanes]
        for w in range(views):
            lanes = slice(w * NCOL, (w + 1) * NCOL)
            shift = off_ref[seg, w]
            value = g[0, w, pl.ds(BASE - 3 + shift, 24), :]
            value = value + g[1, w, pl.ds(BASE - 2 + shift, 24), :]
            value = value + g[2, w, pl.ds(BASE - 1 + shift, 24), :]
            xa[:, lanes] = jnp.where(inside, value, 0.0)
        xf[0:2, :] = ext[ef, 0:16, :].astype(F32)[14:16, :]
        xf[2 : 2 + rows, :] = ext[ef, 16:32, :].astype(F32)
        xf[rows + 2 : rows + 4, :] = ext[ef, 32:48, :].astype(F32)[0:2, :]
        dual[...] += network(
            [read_u, rows_of(xa), rows_of(xs)], dual_steps, dual_keeps, 24, wd, cold, vd, 3
        )
        send(eh, dual)
        receive(eh)
        for w in range(views):
            lanes = slice(w * NCOL, (w + 1) * NCOL)
            u[w, 8:56, :] = ext[eh, 0:48, lanes].astype(F32)
            u[w, 6:8, :] = far_r[eh, 0, :, lanes].astype(F32)
            u[w, 56:58, :] = far_r[eh, 1, :, lanes].astype(F32)
        back = None
        for k in range(3):
            window = jnp.concatenate(
                [
                    u[w, pl.ds(BASE - 1 - k - off_ref[seg, w], 24), :]
                    for w in range(views)
                ],
                1,
            ).astype(BF)
            part = lax.dot_general(
                window, proj[k], (((1,), (1,)), ((), ())), preferred_element_type=F32
            )
            back = part if back is None else back + part
        xa[...] = jnp.where(inside, back, 0.0)
        field[...] += network(
            [rows_of(xf), rows_of(xa)], primal_steps, primal_keeps, 16, wp, colp, vp, 9
        )

        @pl.when(it < ITERS - 1)
        def _():
            send(ef + 2, field)

        return carry

    lax.fori_loop(0, ITERS, iteration, 0)
    out_ref[0] = field[...]


def per_device(
    start_volume, sinogram, offsets, projector, dual_in, dual_out, primal_in, primal_out
):
    _, rows, cells = start_volume.shape
    seg_count = lax.axis_size("segment")
    gz_count = lax.axis_size("gz")
    sizes = (seg_count, gz_count, rows, cells)
    exchanges = 2 * ITERS
    any_spec = pl.BlockSpec(memory_space=pl.ANY)
    vm = pltpu.VMEM
    return pl.pallas_call(
        functools.partial(kernel, sizes),
        out_shape=jax.ShapeDtypeStruct((1, rows, cells), F32),
        in_specs=[any_spec, any_spec, pl.BlockSpec(memory_space=pltpu.SMEM)] + [any_spec] * 5,
        out_specs=pl.BlockSpec(memory_space=pltpu.VMEM),
        scratch_shapes=[
            vm((rows, cells), F32),
            vm((rows, cells), F32),
            vm((rows, cells), F32),
            vm(projector.shape, BF),
            vm(dual_in.shape, BF),
            vm(dual_out.shape, BF),
            vm(primal_in.shape, BF),
            vm(primal_out.shape, BF),
            vm((exchanges, 64, cells), BF),
            vm((exchanges, 2, 2, cells), BF),
            vm((exchanges, 2, 2, cells), BF),
            vm((2, 2, cells), BF),
            vm((2, 2, cells), BF),
            vm((16, cells), F32),
            vm((3, cells // NCOL, 64, NCOL), F32),
            vm((cells // NCOL, 64, NCOL), F32),
            vm((24, cells), F32),
            vm((24, cells), F32),
            vm((24, cells), F32),
            vm((6 * 32, 80), BF),
            vm((3 * rows, 640), BF),
            vm((6 * 64, 144), BF),
            vm((9 * rows, 1152), BF),
            vm((GROUPS, 80, cells), BF),
            vm((GROUPS, 144, cells), BF),
            vm((1152, 256), BF),
            vm((9 * rows, cells), F32),
            pltpu.SemaphoreType.DMA((7,)),
            pltpu.SemaphoreType.DMA((exchanges, 4)),
            pltpu.SemaphoreType.DMA((exchanges, 4)),
            pltpu.SemaphoreType.DMA((2,)),
            pltpu.SemaphoreType.DMA((2,)),
        ],
        compiler_params=pltpu.CompilerParams(
            collective_id=0, has_side_effects=True, vmem_limit_bytes=60 * 1024 * 1024
        ),
        name="reconstruct",
    )(start_volume, sinogram, offsets, projector, dual_in, dual_out, primal_in, primal_out)


def solution(mesh):
    in_specs = (P(None, "gz", None), P(None, "gz", None), P(), P(), P(), P(), P(), P())
    out_specs = P("segment", "gz", None)
    return jax.shard_map(
        per_device, mesh=mesh, in_specs=in_specs, out_specs=out_specs, check_vma=False
    )
```
